32 devices in a mesh: freq: 4 (over y, x), tile: 8 (over z, core).
Axes of the slice: x: 2, y: 2, z: 4, core: 2. Of those that a mesh axis runs over, the one named last changes fastest.
Arguments:
- traces: bfloat16 [256, 8192, 128], P('freq', 'tile'), may hold values from -6 to 6
- right_basis: bfloat16 [16, 8192, 4096], P('freq', 'tile'), may hold values from -0.25 to 0.25
- left_basis: bfloat16 [16, 8192, 4096], P('freq', 'tile'), may hold values from -0.09375 to 0.09375
- tile_ranks: int32 [16, 32, 32], P('freq'), may hold values from 8 to 64, as said below
Outputs:
- wavefield: bfloat16 [16, 2, 8192, 128], P('freq', None, 'tile')
The draws below stay inside these ranges and needn't reach their ends.
Inputs may be any that keep to these rules, and one draw needn't show every extreme that they name: `tile_ranks`: diagonal tiles have rank 64; the ranks of the other tiles are drawn independently of the tile's position, evenly over the whole range.
All inputs are finite; a program needn't handle non-finite values.
Results may differ from the reference program's by a relative error of at most 0.015.
Values may be sent and summed in bfloat16 or wider, within the bound.
A program may use at most 320 MiB of HBM per device.

```python
import math
import jax
import jax.numpy as jnp
from jax import lax

N = 8192
TB = 256
R = 64
S = 128
NF = 16
NT = 256
NB = 32
N_TILE = 8


def draw_tile_ranks(key, part):
    tile_index = jnp.arange(NB, dtype=jnp.int32)
    lowest = max(R // 8, 1)
    rank_value = jax.random.randint(key, (NF, NB, NB), lowest, R + 1, dtype=jnp.int32)
    on_diagonal = tile_index[:, None] == tile_index[None, :]
    rank_value = jnp.where(on_diagonal[None], R, rank_value)
    return rank_value.astype(jnp.int32)


def shard_levels(key, shape, pieces, least, high):
    factor_of, own = 1.0, jax.random.fold_in(key, 6)
    for position, blocks in pieces:
        heights = jnp.exp(jax.random.uniform(jax.random.fold_in(own, position), (blocks,), jnp.float32, least / len(pieces), high / len(pieces)))
        factor_of = factor_of * jnp.repeat(heights, shape[position] // blocks).reshape([-1 if axis == position else 1 for axis in range(len(shape))])
    return factor_of


def normal_values(rng, shape, scale, most, shards=(), kind=jnp.bfloat16):
    result = jax.random.normal(rng, shape, jnp.float32) * scale
    if len(shards) > 0:
        result = shard_levels(rng, shape, shards, -0.22, 0.18) * result
    return jnp.clip(result, min=-most, max=most).astype(kind)


def setup_inputs(seed: int = 0) -> dict:
    key_of = jax.random.split(jax.random.key(seed), 5)
    traces = normal_values(key_of[0], (NT, N, S), 1.0, 6.0, ((0, 4), (1, 8)))
    right_basis = normal_values(key_of[1], (NF, N, 2 * NB * R), (2 * TB) ** -0.5, 0.25, ((0, 4), (1, 8)))
    left_basis = normal_values(key_of[2], (NF, N, 2 * NB * R), (2 * NB * R) ** -0.5, 0.09375, ((0, 4), (1, 8)))
    tile_ranks = draw_tile_ranks(jax.random.fold_in(key_of[4], 71), 0)
    return dict(traces=traces, right_basis=right_basis, left_basis=left_basis, tile_ranks=tile_ranks)


def twiddles(freq_ids, time_ids, total_time):
    phase_int = freq_ids[:, None] * time_ids[None, :] % total_time
    angle_rad = phase_int.astype(jnp.float32) * (2.0 * math.pi / total_time)
    factor = 1.0 / math.sqrt(total_time)
    return jnp.stack([jnp.cos(angle_rad) * factor, -jnp.sin(angle_rad) * factor], 1).astype(jnp.bfloat16)

def reference(traces, right_basis, left_basis, tile_ranks):
    tile_rows = N // TB
    grid_rows = N // N_TILE
    piece_rows = min(TB, grid_rows)
    piece_count = N // piece_rows
    per_tile = max(TB // grid_rows, 1)
    flat_traces = traces.reshape(NT, N * S)
    time_ids = jnp.arange(NT, dtype=jnp.int32)
    column_ids = jnp.arange(piece_count, dtype=jnp.int32) // per_tile

    def one_freq(inputs):
        freq_index, right_freq, left_freq, ranks_freq = inputs
        twiddle = twiddles(jnp.reshape(freq_index + 1, (1,)).astype(jnp.int32), time_ids, NT)[0]
        spectra = jnp.dot(twiddle, flat_traces, preferred_element_type=jnp.float32).astype(jnp.bfloat16)
        spectra = spectra.reshape(2, piece_count, piece_rows, S)
        right_pieces = right_freq.reshape(piece_count, piece_rows, 2 * tile_rows * R)
        products = jnp.einsum('qnc,pqns->cqps', right_pieces.astype(jnp.float32), spectra.astype(jnp.float32))
        products = products.reshape(2, tile_rows, R, piece_count, 2, S)
        real_part = products[0, :, :, :, 0] - products[1, :, :, :, 1]
        imag_part = products[0, :, :, :, 1] + products[1, :, :, :, 0]
        stacked = jnp.transpose(jnp.stack([real_part, imag_part], 0), (3, 1, 0, 2, 4))
        chosen = ranks_freq[:, column_ids]
        keep_rows = jnp.arange(R, dtype=jnp.int32)[None, None, :] < jnp.transpose(chosen)[:, :, None]
        rank_rows = jnp.where(keep_rows[:, :, None, :, None], stacked, jnp.float32(0.0)).astype(jnp.bfloat16)
        grouped = rank_rows.astype(jnp.float32).reshape(tile_rows, per_tile, tile_rows, 2, R, S)
        coupled = lax.optimization_barrier(jnp.sum(grouped, axis=1)).astype(jnp.bfloat16)
        by_row = jnp.transpose(coupled, (1, 0, 2, 3, 4))
        real_coupled = by_row[:, :, 0]
        imag_coupled = by_row[:, :, 1]
        upper_half = jnp.stack([real_coupled, imag_coupled], -2)
        lower_half = jnp.stack([-imag_coupled, real_coupled], -2)
        operand = jnp.stack([upper_half, lower_half], 1)
        left_tiles = left_freq.reshape(tile_rows, TB, 2, tile_rows, R)
        field_out = jnp.einsum('itajk,iajkys->yits', left_tiles.astype(jnp.float32), operand.astype(jnp.float32))
        return field_out.reshape(2, N, S).astype(jnp.bfloat16)
    return lax.map(one_freq, (jnp.arange(NF, dtype=jnp.int32), right_basis, left_basis, tile_ranks))
```

```python
import functools
import math

import jax
import jax.numpy as jnp
from jax import lax
from jax.experimental import pallas as pl
from jax.experimental.pallas import tpu as pltpu
from jax.sharding import PartitionSpec as P


def twiddles(freq_ids, time_ids, total_time):
    phase_int = freq_ids[:, None] * time_ids[None, :] % total_time
    angle_rad = phase_int.astype(jnp.float32) * (2.0 * math.pi / total_time)
    factor = 1.0 / math.sqrt(total_time)
    return jnp.stack([jnp.cos(angle_rad) * factor, -jnp.sin(angle_rad) * factor], 1).astype(
        jnp.bfloat16
    )


def send_pieces(rank_rows, tile_count, tile_rows, per_tile):
    freq_dev = rank_rows.shape[1]
    rank_max = rank_rows.shape[4]
    sources = rank_rows.shape[5]
    if tile_rows < tile_count:
        copies = tile_count // tile_rows
        outgoing = jnp.broadcast_to(rank_rows[:, None], (tile_rows, copies) + rank_rows.shape[1:])
        outgoing = outgoing.reshape((tile_count,) + rank_rows.shape[1:])
    else:
        outgoing = rank_rows
    received = lax.all_to_all(outgoing, "tile", split_axis=0, concat_axis=2, tiled=True)
    row_tiles = received.shape[0]
    grouped = received.reshape(row_tiles, freq_dev, tile_rows, per_tile, 2, rank_max, sources)
    return jnp.sum(grouped.astype(jnp.float32), axis=3).astype(jnp.bfloat16)


def split_tiles_body(traces, right_basis, left_basis, tile_ranks):
    freq_count = lax.axis_size("freq")
    tile_count = lax.axis_size("tile")
    time_rows, grid_rows, sources = traces.shape
    freq_dev = right_basis.shape[0]
    total_time = time_rows * freq_count
    tile_rows = tile_ranks.shape[1]
    rank_max = right_basis.shape[2] // (2 * tile_rows)
    tile_points = grid_rows * tile_count // tile_rows
    freq_ids = 1 + jnp.arange(freq_count * freq_dev, dtype=jnp.int32)
    time_ids = lax.axis_index("freq") * time_rows + jnp.arange(time_rows, dtype=jnp.int32)
    twiddle = twiddles(freq_ids, time_ids, total_time)
    spectra = lax.psum_scatter(
        jnp.einsum("fpt,tns->fpns", twiddle, traces, preferred_element_type=jnp.float32).astype(
            jnp.bfloat16
        ),
        "freq",
        scatter_dimension=0,
        tiled=True,
    )
    piece_rows = min(tile_points, grid_rows)
    pieces_dev = grid_rows // piece_rows
    per_tile = max(tile_points // grid_rows, 1)
    spectra_pieces = spectra.reshape(freq_dev, 2, pieces_dev, piece_rows, sources)
    right_pieces = right_basis.reshape(freq_dev, pieces_dev, piece_rows, 2 * tile_rows * rank_max)
    products = jnp.einsum(
        "fqnc,fpqns->cfqps", right_pieces, spectra_pieces, preferred_element_type=jnp.float32
    )
    products = products.reshape(2, tile_rows, rank_max, freq_dev, pieces_dev, 2, sources)
    real_part = products[0, :, :, :, :, 0] - products[1, :, :, :, :, 1]
    imag_part = products[0, :, :, :, :, 1] + products[1, :, :, :, :, 0]
    stacked = jnp.transpose(jnp.stack([real_part, imag_part], 0), (1, 3, 4, 0, 2, 5))
    column_ids = (
        lax.axis_index("tile") * pieces_dev + jnp.arange(pieces_dev, dtype=jnp.int32)
    ) // per_tile
    onehot = (column_ids[:, None] == jnp.arange(tile_rows, dtype=jnp.int32)[None, :]).astype(
        jnp.int32
    )
    chosen = jnp.sum(tile_ranks[:, :, None, :] * onehot[None, None], axis=-1)
    keep_rows = jnp.arange(rank_max, dtype=jnp.int32)[None, None, None, :] < chosen[..., None]
    keep_rows = jnp.transpose(keep_rows, (1, 0, 2, 3))[:, :, :, None, :, None]
    rank_rows = jnp.where(keep_rows, stacked, jnp.float32(0.0)).astype(jnp.bfloat16)
    coupled = send_pieces(rank_rows, tile_count, tile_rows, per_tile)
    row_tiles = coupled.shape[0]
    rows_tile = grid_rows // row_tiles
    real_coupled = coupled[:, :, :, 0]
    imag_coupled = coupled[:, :, :, 1]
    upper_half = jnp.stack([real_coupled, imag_coupled], -2)
    lower_half = jnp.stack([-imag_coupled, real_coupled], -2)
    operand = jnp.stack([upper_half, lower_half], 2)
    left_tiles = left_basis.reshape(freq_dev, row_tiles, rows_tile, 2, tile_rows, rank_max)
    field_out = jnp.einsum(
        "frtajk,rfajkys->fyrts", left_tiles, operand, preferred_element_type=jnp.float32
    )
    return field_out.reshape(freq_dev, 2, grid_rows, sources).astype(jnp.bfloat16)


def pack_kernel(dims, off_ref, rank_ref, me_ref, right_ref, spec_ref, out_ref, own_ref, buf):
    peers, per_dev, rank, sources, cap, full = dims
    freq, col = pl.program_id(0), pl.program_id(1)
    half = peers * per_dev * rank
    real, imag = spec_ref[0, 0], spec_ref[0, 1]
    upper = jnp.concatenate([real, imag], axis=1)
    lower = jnp.concatenate([-imag, real], axis=1)
    rows = lax.broadcasted_iota(jnp.int32, (rank, 2 * sources), 0)
    contract = (((0,), (0,)), ((), ()))
    width = per_dev * rank
    for peer in range(peers):
        real_cols = right_ref[0, :, peer * width : (peer + 1) * width]
        imag_cols = right_ref[0, :, half + peer * width : half + (peer + 1) * width]
        total = lax.dot_general(real_cols, upper, contract, preferred_element_type=jnp.float32)
        total += lax.dot_general(imag_cols, lower, contract, preferred_element_type=jnp.float32)
        for row in range(per_dev):
            index = ((freq * per_dev + col) * peers + peer) * per_dev + row
            kept = jnp.where(rows < rank_ref[index], total[row * rank : (row + 1) * rank], 0.0)
            buf[0, peer, pl.ds(off_ref[index], rank), :] = kept[:, :sources]
            buf[1, peer, pl.ds(off_ref[index], rank), :] = kept[:, sources:]

    @pl.when((freq == pl.num_programs(0) - 1) & (col == pl.num_programs(1) - 1))
    def _():
        @pl.loop(0, peers)
        def _(peer):
            for part in range(2):
                lanes = slice(part * sources, (part + 1) * sources)
                out_ref[peer, :, lanes] = buf[part, peer, :cap, :].astype(out_ref.dtype)

        for part in range(2):
            lanes = slice(part * sources, (part + 1) * sources)
            own_ref[:, lanes] = buf[part, me_ref[0], :full, :].astype(own_ref.dtype)


def unpack_kernel(dims, off_ref, rank_ref, me_ref, recv_ref, own_ref, left_ref, out_ref, buf, operand):
    peers, per_dev, rank, sources, cap, full = dims
    freq, row = pl.program_id(0), pl.program_id(1)
    half = peers * per_dev * rank

    @pl.when((freq == 0) & (row == 0))
    def _():
        @pl.loop(0, peers)
        def _(peer):
            for part in range(2):
                lanes = slice(part * sources, (part + 1) * sources)
                buf[part, peer, :cap, :] = recv_ref[peer, :, lanes].astype(jnp.float32)

        for part in range(2):
            lanes = slice(part * sources, (part + 1) * sources)
            buf[part, me_ref[0], :full, :] = own_ref[:, lanes].astype(jnp.float32)

    rows = lax.broadcasted_iota(jnp.int32, (rank, sources), 0)
    for col in range(peers * per_dev):
        index = (freq * per_dev + row) * (peers * per_dev) + col
        window = pl.ds(off_ref[index], rank)
        keep = rows < rank_ref[index]
        real = jnp.where(keep, buf[0, col // per_dev, window, :], 0.0)
        imag = jnp.where(keep, buf[1, col // per_dev, window, :], 0.0)
        upper = slice(col * rank, (col + 1) * rank)
        lower = slice(half + col * rank, half + (col + 1) * rank)
        operand[upper, :sources] = real.astype(operand.dtype)
        operand[upper, sources:] = imag.astype(operand.dtype)
        operand[lower, :sources] = (-imag).astype(operand.dtype)
        operand[lower, sources:] = real.astype(operand.dtype)
    field = jnp.dot(left_ref[0], operand[...], preferred_element_type=jnp.float32)
    out_ref[0, 0] = field[:, :sources].astype(out_ref.dtype)
    out_ref[0, 1] = field[:, sources:].astype(out_ref.dtype)


def pack(dims, first, count, offsets, ranks, me, right_basis, spectra):
    peers, per_dev, rank, sources, cap, full = dims
    points = right_basis.shape[1] // per_dev
    width = right_basis.shape[2]
    return pl.pallas_call(
        functools.partial(pack_kernel, dims),
        out_shape=(
            jax.ShapeDtypeStruct((peers, cap, 2 * sources), jnp.bfloat16),
            jax.ShapeDtypeStruct((full, 2 * sources), jnp.bfloat16),
        ),
        grid_spec=pltpu.PrefetchScalarGridSpec(
            num_scalar_prefetch=3,
            grid=(count, per_dev),
            in_specs=[
                pl.BlockSpec((1, points, width), lambda f, j, *_: (f + first, j, 0)),
                pl.BlockSpec((1, 2, points, sources), lambda f, j, *_: (f, 0, j, 0)),
            ],
            out_specs=[
                pl.BlockSpec((peers, cap, 2 * sources), lambda f, j, *_: (0, 0, 0)),
                pl.BlockSpec((full, 2 * sources), lambda f, j, *_: (0, 0)),
            ],
            scratch_shapes=[pltpu.VMEM((2, peers, full + rank, sources), jnp.float32)],
        ),
        compiler_params=pltpu.CompilerParams(vmem_limit_bytes=62 << 20),
        cost_estimate=pl.CostEstimate(
            flops=4 * count * per_dev * points * width * sources,
            bytes_accessed=2 * count * per_dev * points * width + 4 * peers * cap * sources,
            transcendentals=0,
        ),
        name="pack_rows",
    )(offsets, ranks, me, right_basis, spectra)


def unpack(dims, first, count, offsets, ranks, me, received, own, left_basis):
    peers, per_dev, rank, sources, cap, full = dims
    grid_rows, width = left_basis.shape[1:]
    points = grid_rows // per_dev
    return pl.pallas_call(
        functools.partial(unpack_kernel, dims),
        out_shape=jax.ShapeDtypeStruct((count, 2, grid_rows, sources), jnp.bfloat16),
        grid_spec=pltpu.PrefetchScalarGridSpec(
            num_scalar_prefetch=3,
            grid=(count, per_dev),
            in_specs=[
                pl.BlockSpec((peers, cap, 2 * sources), lambda f, i, *_: (0, 0, 0)),
                pl.BlockSpec((full, 2 * sources), lambda f, i, *_: (0, 0)),
                pl.BlockSpec((1, points, width), lambda f, i, *_: (f + first, i, 0)),
            ],
            out_specs=pl.BlockSpec((1, 2, points, sources), lambda f, i, *_: (f, 0, i, 0)),
            scratch_shapes=[
                pltpu.VMEM((2, peers, full + rank, sources), jnp.float32),
                pltpu.VMEM((width, 2 * sources), jnp.bfloat16),
            ],
        ),
        compiler_params=pltpu.CompilerParams(vmem_limit_bytes=62 << 20),
        cost_estimate=pl.CostEstimate(
            flops=4 * count * grid_rows * width * sources,
            bytes_accessed=2 * count * grid_rows * width + 4 * peers * cap * sources,
            transcendentals=0,
        ),
        name="apply_left",
    )(offsets, ranks, me, received, own, left_basis)


def tile_order(ranks, peers, per_dev):
    count = ranks.shape[0]
    split = ranks.reshape(count, peers, per_dev, peers, per_dev)
    return jnp.transpose(split, (3, 1, 0, 4, 2)).reshape(peers, peers, count * per_dev * per_dev)


def pipeline(chunks, packed, traces, right_basis, left_basis, tile_ranks):
    freq_count = lax.axis_size("freq")
    peers = lax.axis_size("tile")
    time_rows, grid_rows, sources = traces.shape
    freq_dev = right_basis.shape[0]
    total_time = time_rows * freq_count
    tile_rows = tile_ranks.shape[1]
    per_dev = tile_rows // peers
    rank = right_basis.shape[2] // (2 * tile_rows)
    time_ids = lax.axis_index("freq") * time_rows + jnp.arange(time_rows, dtype=jnp.int32)
    me = lax.axis_index("tile").astype(jnp.int32)
    fields = []
    for first, count, cap in chunks:
        freq_ids = (
            1
            + jnp.arange(freq_count, dtype=jnp.int32)[:, None] * freq_dev
            + jnp.arange(first, first + count, dtype=jnp.int32)[None, :]
        ).reshape(freq_count * count)
        partial_sums = jnp.einsum(
            "fpt,tns->fpns",
            twiddles(freq_ids, time_ids, total_time),
            traces,
            preferred_element_type=jnp.float32,
        ).astype(jnp.bfloat16)
        spectra = lax.psum_scatter(partial_sums, "freq", scatter_dimension=0, tiled=True)
        ranks = tile_order(tile_ranks[first : first + count], peers, per_dev)
        full = count * per_dev * per_dev * rank
        if packed:
            offsets = jnp.cumsum(ranks, axis=2) - ranks
        else:
            offsets = jnp.broadcast_to(
                jnp.arange(ranks.shape[2], dtype=jnp.int32) * rank, ranks.shape
            )
        dims = (peers, per_dev, rank, sources, cap, full)

        def outgoing(table):
            mine = lax.dynamic_index_in_dim(table, me, 0, keepdims=False)
            mine = mine.reshape(peers, count, per_dev, per_dev)
            return jnp.transpose(mine, (1, 2, 0, 3)).reshape(-1)

        def incoming(table):
            mine = lax.dynamic_index_in_dim(table, me, 1, keepdims=False)
            mine = mine.reshape(peers, count, per_dev, per_dev)
            return jnp.transpose(mine, (1, 3, 0, 2)).reshape(-1)

        sent, own = pack(
            dims, first, count, outgoing(offsets), outgoing(ranks), me[None], right_basis, spectra
        )
        received = lax.all_to_all(sent, "tile", split_axis=0, concat_axis=0, tiled=True)
        fields.append(
            unpack(
                dims, first, count, incoming(offsets), incoming(ranks), me[None], received, own,
                left_basis,
            )
        )
    return jnp.concatenate(fields, axis=0)


def body(traces, right_basis, left_basis, tile_ranks):
    peers = lax.axis_size("tile")
    tile_rows = tile_ranks.shape[1]
    if tile_rows % peers != 0:
        return split_tiles_body(traces, right_basis, left_basis, tile_ranks)
    freq_dev = right_basis.shape[0]
    rank = right_basis.shape[2] // (2 * tile_rows)
    full = (tile_rows // peers) ** 2 * rank
    chunks = [(first, 1, full) for first in range(freq_dev)]
    return pipeline(chunks, False, traces, right_basis, left_basis, tile_ranks)


def solution(mesh):
    return jax.shard_map(
        body,
        mesh=mesh,
        in_specs=(
            P("freq", "tile", None),
            P("freq", "tile", None),
            P("freq", "tile", None),
            P("freq", None, None),
        ),
        out_specs=P("freq", None, "tile", None),
        check_vma=False,
    )
```

```python
import functools
import math

import jax
import jax.numpy as jnp
from jax import lax
from jax.experimental import pallas as pl
from jax.experimental.pallas import tpu as pltpu
from jax.sharding import PartitionSpec as P


def twiddles(freq_ids, time_ids, total_time):
    phase_int = freq_ids[:, None] * time_ids[None, :] % total_time
    angle_rad = phase_int.astype(jnp.float32) * (2.0 * math.pi / total_time)
    factor = 1.0 / math.sqrt(total_time)
    return jnp.stack([jnp.cos(angle_rad) * factor, -jnp.sin(angle_rad) * factor], 1).astype(
        jnp.bfloat16
    )


def send_pieces(rank_rows, tile_count, tile_rows, per_tile):
    freq_dev = rank_rows.shape[1]
    rank_max = rank_rows.shape[4]
    sources = rank_rows.shape[5]
    if tile_rows < tile_count:
        copies = tile_count // tile_rows
        outgoing = jnp.broadcast_to(rank_rows[:, None], (tile_rows, copies) + rank_rows.shape[1:])
        outgoing = outgoing.reshape((tile_count,) + rank_rows.shape[1:])
    else:
        outgoing = rank_rows
    received = lax.all_to_all(outgoing, "tile", split_axis=0, concat_axis=2, tiled=True)
    row_tiles = received.shape[0]
    grouped = received.reshape(row_tiles, freq_dev, tile_rows, per_tile, 2, rank_max, sources)
    return jnp.sum(grouped.astype(jnp.float32), axis=3).astype(jnp.bfloat16)


def split_tiles_body(traces, right_basis, left_basis, tile_ranks):
    freq_count = lax.axis_size("freq")
    tile_count = lax.axis_size("tile")
    time_rows, grid_rows, sources = traces.shape
    freq_dev = right_basis.shape[0]
    total_time = time_rows * freq_count
    tile_rows = tile_ranks.shape[1]
    rank_max = right_basis.shape[2] // (2 * tile_rows)
    tile_points = grid_rows * tile_count // tile_rows
    freq_ids = 1 + jnp.arange(freq_count * freq_dev, dtype=jnp.int32)
    time_ids = lax.axis_index("freq") * time_rows + jnp.arange(time_rows, dtype=jnp.int32)
    twiddle = twiddles(freq_ids, time_ids, total_time)
    spectra = lax.psum_scatter(
        jnp.einsum("fpt,tns->fpns", twiddle, traces, preferred_element_type=jnp.float32).astype(
            jnp.bfloat16
        ),
        "freq",
        scatter_dimension=0,
        tiled=True,
    )
    piece_rows = min(tile_points, grid_rows)
    pieces_dev = grid_rows // piece_rows
    per_tile = max(tile_points // grid_rows, 1)
    spectra_pieces = spectra.reshape(freq_dev, 2, pieces_dev, piece_rows, sources)
    right_pieces = right_basis.reshape(freq_dev, pieces_dev, piece_rows, 2 * tile_rows * rank_max)
    products = jnp.einsum(
        "fqnc,fpqns->cfqps", right_pieces, spectra_pieces, preferred_element_type=jnp.float32
    )
    products = products.reshape(2, tile_rows, rank_max, freq_dev, pieces_dev, 2, sources)
    real_part = products[0, :, :, :, :, 0] - products[1, :, :, :, :, 1]
    imag_part = products[0, :, :, :, :, 1] + products[1, :, :, :, :, 0]
    stacked = jnp.transpose(jnp.stack([real_part, imag_part], 0), (1, 3, 4, 0, 2, 5))
    column_ids = (
        lax.axis_index("tile") * pieces_dev + jnp.arange(pieces_dev, dtype=jnp.int32)
    ) // per_tile
    onehot = (column_ids[:, None] == jnp.arange(tile_rows, dtype=jnp.int32)[None, :]).astype(
        jnp.int32
    )
    chosen = jnp.sum(tile_ranks[:, :, None, :] * onehot[None, None], axis=-1)
    keep_rows = jnp.arange(rank_max, dtype=jnp.int32)[None, None, None, :] < chosen[..., None]
    keep_rows = jnp.transpose(keep_rows, (1, 0, 2, 3))[:, :, :, None, :, None]
    rank_rows = jnp.where(keep_rows, stacked, jnp.float32(0.0)).astype(jnp.bfloat16)
    coupled = send_pieces(rank_rows, tile_count, tile_rows, per_tile)
    row_tiles = coupled.shape[0]
    rows_tile = grid_rows // row_tiles
    real_coupled = coupled[:, :, :, 0]
    imag_coupled = coupled[:, :, :, 1]
    upper_half = jnp.stack([real_coupled, imag_coupled], -2)
    lower_half = jnp.stack([-imag_coupled, real_coupled], -2)
    operand = jnp.stack([upper_half, lower_half], 2)
    left_tiles = left_basis.reshape(freq_dev, row_tiles, rows_tile, 2, tile_rows, rank_max)
    field_out = jnp.einsum(
        "frtajk,rfajkys->fyrts", left_tiles, operand, preferred_element_type=jnp.float32
    )
    return field_out.reshape(freq_dev, 2, grid_rows, sources).astype(jnp.bfloat16)


def pack_kernel(dims, off_ref, rank_ref, place_ref, right_ref, spec_ref, out_ref, own_ref, buf):
    peers, per_dev, rank, sources, cap, full = dims
    freq, col = pl.program_id(0), pl.program_id(1)
    half = peers * per_dev * rank
    real, imag = spec_ref[0, 0], spec_ref[0, 1]
    upper = jnp.concatenate([real, imag], axis=1)
    lower = jnp.concatenate([-imag, real], axis=1)
    rows = lax.broadcasted_iota(jnp.int32, (rank, 2 * sources), 0)
    contract = (((0,), (0,)), ((), ()))
    width = per_dev * rank
    for peer in range(peers):
        real_cols = right_ref[0, :, peer * width : (peer + 1) * width]
        imag_cols = right_ref[0, :, half + peer * width : half + (peer + 1) * width]
        total = lax.dot_general(real_cols, upper, contract, preferred_element_type=jnp.float32)
        total += lax.dot_general(imag_cols, lower, contract, preferred_element_type=jnp.float32)
        for row in range(per_dev):
            index = ((freq * per_dev + col) * peers + peer) * per_dev + row
            kept = jnp.where(rows < rank_ref[index], total[row * rank : (row + 1) * rank], 0.0)
            buf[0, peer, pl.ds(off_ref[index], rank), :] = kept[:, :sources]
            buf[1, peer, pl.ds(off_ref[index], rank), :] = kept[:, sources:]

    @pl.when((freq == pl.num_programs(0) - 1) & (col == pl.num_programs(1) - 1))
    def _():
        @pl.loop(0, peers)
        def _(peer):
            for part in range(2):
                lanes = slice(part * sources, (part + 1) * sources)
                out_ref[peer, :, lanes] = buf[part, peer, :cap, :].astype(out_ref.dtype)

        for part in range(2):
            lanes = slice(part * sources, (part + 1) * sources)
            own_ref[:, lanes] = buf[part, place_ref[0], :full, :].astype(own_ref.dtype)


def unpack_kernel(dims, off_ref, rank_ref, place_ref, recv_ref, own_ref, left_ref, out_ref, buf, operand):
    peers, per_dev, rank, sources, cap, full = dims
    freq, row = pl.program_id(0), pl.program_id(1)
    half = peers * per_dev * rank

    @pl.when((freq == 0) & (row == 0))
    def _():
        @pl.loop(0, peers)
        def _(peer):
            for part in range(2):
                lanes = slice(part * sources, (part + 1) * sources)
                buf[part, peer, :cap, :] = recv_ref[peer, :, lanes].astype(jnp.float32)

        for part in range(2):
            lanes = slice(part * sources, (part + 1) * sources)
            buf[part, place_ref[0], :full, :] = own_ref[:, lanes].astype(jnp.float32)

    rows = lax.broadcasted_iota(jnp.int32, (rank, sources), 0)

    @pl.loop(0, peers, unroll=2)
    def _(peer):
        for each in range(per_dev):
            col = peer * per_dev + each
            index = (freq * per_dev + row) * (peers * per_dev) + col
            window = pl.ds(off_ref[index], rank)
            keep = rows < rank_ref[index]
            real = jnp.where(keep, buf[0, peer, window, :], 0.0)
            imag = jnp.where(keep, buf[1, peer, window, :], 0.0)
            upper = pl.ds(pl.multiple_of(col * rank, rank), rank)
            lower = pl.ds(pl.multiple_of(half + col * rank, rank), rank)
            operand[upper, :sources] = real.astype(operand.dtype)
            operand[upper, sources:] = imag.astype(operand.dtype)
            operand[lower, :sources] = (-imag).astype(operand.dtype)
            operand[lower, sources:] = real.astype(operand.dtype)

    field = jnp.dot(left_ref[0], operand[...], preferred_element_type=jnp.float32)
    out_ref[0, 0] = field[:, :sources].astype(out_ref.dtype)
    out_ref[0, 1] = field[:, sources:].astype(out_ref.dtype)


def pack(dims, count, offsets, ranks, place, right_basis, spectra):
    peers, per_dev, rank, sources, cap, full = dims
    points = right_basis.shape[1] // per_dev
    width = right_basis.shape[2]
    return pl.pallas_call(
        functools.partial(pack_kernel, dims),
        out_shape=(
            jax.ShapeDtypeStruct((peers, cap, 2 * sources), jnp.bfloat16),
            jax.ShapeDtypeStruct((full, 2 * sources), jnp.bfloat16),
        ),
        grid_spec=pltpu.PrefetchScalarGridSpec(
            num_scalar_prefetch=3,
            grid=(count, per_dev),
            in_specs=[
                pl.BlockSpec((1, points, width), lambda f, j, o, r, place: (f + place[1], j, 0)),
                pl.BlockSpec((1, 2, points, sources), lambda f, j, *_: (f, 0, j, 0)),
            ],
            out_specs=[
                pl.BlockSpec((peers, cap, 2 * sources), lambda f, j, *_: (0, 0, 0)),
                pl.BlockSpec((full, 2 * sources), lambda f, j, *_: (0, 0)),
            ],
            scratch_shapes=[pltpu.VMEM((2, peers, full + rank, sources), jnp.float32)],
        ),
        compiler_params=pltpu.CompilerParams(vmem_limit_bytes=62 << 20),
        cost_estimate=pl.CostEstimate(
            flops=4 * count * per_dev * points * width * sources,
            bytes_accessed=2 * count * per_dev * points * width + 4 * peers * cap * sources,
            transcendentals=0,
        ),
        name="pack_rows",
    )(offsets, ranks, place, right_basis, spectra)


def unpack(dims, count, offsets, ranks, place, received, own, left_basis):
    peers, per_dev, rank, sources, cap, full = dims
    grid_rows, width = left_basis.shape[1:]
    points = grid_rows // per_dev
    return pl.pallas_call(
        functools.partial(unpack_kernel, dims),
        out_shape=jax.ShapeDtypeStruct((count, 2, grid_rows, sources), jnp.bfloat16),
        grid_spec=pltpu.PrefetchScalarGridSpec(
            num_scalar_prefetch=3,
            grid=(count, per_dev),
            in_specs=[
                pl.BlockSpec((peers, cap, 2 * sources), lambda f, i, *_: (0, 0, 0)),
                pl.BlockSpec((full, 2 * sources), lambda f, i, *_: (0, 0)),
                pl.BlockSpec((1, points, width), lambda f, i, o, r, place: (f + place[1], i, 0)),
            ],
            out_specs=pl.BlockSpec((1, 2, points, sources), lambda f, i, *_: (f, 0, i, 0)),
            scratch_shapes=[
                pltpu.VMEM((2, peers, full + rank, sources), jnp.float32),
                pltpu.VMEM((width, 2 * sources), jnp.bfloat16),
            ],
        ),
        compiler_params=pltpu.CompilerParams(vmem_limit_bytes=62 << 20),
        cost_estimate=pl.CostEstimate(
            flops=4 * count * grid_rows * width * sources,
            bytes_accessed=2 * count * grid_rows * width + 4 * peers * cap * sources,
            transcendentals=0,
        ),
        name="apply_left",
    )(offsets, ranks, place, received, own, left_basis)


def tile_order(ranks, peers, per_dev):
    count = ranks.shape[0]
    split = ranks.reshape(count, peers, per_dev, peers, per_dev)
    return jnp.transpose(split, (3, 1, 0, 4, 2)).reshape(peers, peers, count * per_dev * per_dev)


def partial_spectra(first, count, freq_dev, traces):
    freq_count = lax.axis_size("freq")
    time_rows = traces.shape[0]
    time_ids = lax.axis_index("freq") * time_rows + jnp.arange(time_rows, dtype=jnp.int32)
    freq_ids = (
        1
        + jnp.arange(freq_count, dtype=jnp.int32)[:, None] * freq_dev
        + (first + jnp.arange(count, dtype=jnp.int32))[None, :]
    ).reshape(freq_count * count)
    return jnp.einsum(
        "fpt,tns->fpns",
        twiddles(freq_ids, time_ids, time_rows * freq_count),
        traces,
        preferred_element_type=jnp.float32,
    ).astype(jnp.bfloat16)


def scatter_spectra(partial_sums):
    return lax.psum_scatter(partial_sums, "freq", scatter_dimension=0, tiled=True)


def tables(first, count, packed, tile_ranks, peers, per_dev, rank):
    ranks = lax.dynamic_slice_in_dim(tile_ranks, first, count, axis=0)
    ranks = tile_order(ranks, peers, per_dev)
    if packed:
        offsets = jnp.cumsum(ranks, axis=2) - ranks
    else:
        offsets = jnp.broadcast_to(jnp.arange(ranks.shape[2], dtype=jnp.int32) * rank, ranks.shape)
    me = lax.axis_index("tile").astype(jnp.int32)

    def outgoing(table):
        mine = lax.dynamic_index_in_dim(table, me, 0, keepdims=False)
        mine = mine.reshape(peers, count, per_dev, per_dev)
        return jnp.transpose(mine, (1, 2, 0, 3)).reshape(-1)

    def incoming(table):
        mine = lax.dynamic_index_in_dim(table, me, 1, keepdims=False)
        mine = mine.reshape(peers, count, per_dev, per_dev)
        return jnp.transpose(mine, (1, 3, 0, 2)).reshape(-1)

    place = jnp.stack([me, jnp.asarray(first, jnp.int32)])
    sending = (outgoing(offsets), outgoing(ranks), place)
    receiving = (incoming(offsets), incoming(ranks), place)
    return sending, receiving


def exchange(sent):
    return lax.all_to_all(sent, "tile", split_axis=0, concat_axis=0, tiled=True)


def body(traces, right_basis, left_basis, tile_ranks):
    peers = lax.axis_size("tile")
    tile_rows = tile_ranks.shape[1]
    if tile_rows % peers != 0:
        return split_tiles_body(traces, right_basis, left_basis, tile_ranks)
    freq_dev = right_basis.shape[0]
    sources = traces.shape[2]
    per_dev = tile_rows // peers
    rank = right_basis.shape[2] // (2 * tile_rows)
    tiles = per_dev * per_dev

    def capacity(count):
        lowest = max(rank // 8, 1)
        mean = (lowest + rank) / 2
        spread = math.sqrt(((rank - lowest + 1) ** 2 - 1) / 12)
        rows = mean * count * tiles + 4.1 * spread * math.sqrt(count * tiles)
        return min(-(-int(rows) // 16) * 16, count * tiles * rank)

    counts = [1] + [2] * ((freq_dev - 2) // 2) + [1] * (1 + freq_dev % 2)
    if freq_dev < 2:
        counts = [1] * freq_dev
    starts = [sum(counts[:n]) for n in range(len(counts))]
    chunks = list(zip(starts, counts))

    elsewhere = ~jnp.eye(peers, dtype=bool)
    over = jnp.int32(0)
    for first, count in chunks:
        totals = jnp.sum(tile_order(tile_ranks[first : first + count], peers, per_dev), axis=2)
        over = over | jnp.any((totals > capacity(count)) & elsewhere).astype(jnp.int32)
    over = lax.pmax(over, "freq")

    spectra = scatter_spectra(partial_spectra(*chunks[0], freq_dev, traces))
    following = None
    if len(chunks) > 1:
        following = partial_spectra(*chunks[1], freq_dev, traces)
        spectra, following = lax.optimization_barrier((spectra, following))

    def fast(spectra, following, traces, right_basis, left_basis, tile_ranks):
        fields = []
        own = None
        for n, (first, count) in enumerate(chunks):
            dims = (peers, per_dev, rank, sources, capacity(count), count * tiles * rank)
            sending, receiving = tables(first, count, True, tile_ranks, peers, per_dev, rank)
            if n > 0:
                sending, _ = lax.optimization_barrier((sending, own))
            upcoming = None
            if n + 1 < len(chunks):
                upcoming = scatter_spectra(following)
            sent, own = pack(dims, count, *sending, right_basis, spectra)
            received = exchange(sent)
            if n + 2 < len(chunks):
                following = partial_spectra(*chunks[n + 2], freq_dev, traces)
                upcoming, following = lax.optimization_barrier((upcoming, following))
            spectra = upcoming
            fields.append(unpack(dims, count, *receiving, received, own, left_basis))
        return jnp.concatenate(fields, axis=0)

    def complete(spectra, following, traces, right_basis, left_basis, tile_ranks):
        full = tiles * rank
        dims = (peers, per_dev, rank, sources, full, full)

        def one(carry, first):
            sending, receiving = tables(first, 1, False, tile_ranks, peers, per_dev, rank)
            spectra = scatter_spectra(partial_spectra(first, 1, freq_dev, traces))
            sent, own = pack(dims, 1, *sending, right_basis, spectra)
            field = unpack(dims, 1, *receiving, exchange(sent), own, left_basis)
            return carry, field[0]

        return lax.scan(one, 0, jnp.arange(freq_dev, dtype=jnp.int32))[1]

    return lax.cond(
        over == 0, fast, complete, spectra, following, traces, right_basis, left_basis, tile_ranks
    )


def solution(mesh):
    return jax.shard_map(
        body,
        mesh=mesh,
        in_specs=(
            P("freq", "tile", None),
            P("freq", "tile", None),
            P("freq", "tile", None),
            P("freq", None, None),
        ),
        out_specs=P("freq", None, "tile", None),
        check_vma=False,
    )
```

```python
import functools
import math

import jax
import jax.numpy as jnp
from jax import lax
from jax.experimental import pallas as pl
from jax.experimental.pallas import tpu as pltpu
from jax.sharding import PartitionSpec as P


def twiddles(freq_ids, time_ids, total_time):
    phase_int = freq_ids[:, None] * time_ids[None, :] % total_time
    angle_rad = phase_int.astype(jnp.float32) * (2.0 * math.pi / total_time)
    factor = 1.0 / math.sqrt(total_time)
    return jnp.stack([jnp.cos(angle_rad) * factor, -jnp.sin(angle_rad) * factor], 1).astype(
        jnp.bfloat16
    )


def send_pieces(rank_rows, tile_count, tile_rows, per_tile):
    freq_dev = rank_rows.shape[1]
    rank_max = rank_rows.shape[4]
    sources = rank_rows.shape[5]
    if tile_rows < tile_count:
        copies = tile_count // tile_rows
        outgoing = jnp.broadcast_to(rank_rows[:, None], (tile_rows, copies) + rank_rows.shape[1:])
        outgoing = outgoing.reshape((tile_count,) + rank_rows.shape[1:])
    else:
        outgoing = rank_rows
    received = lax.all_to_all(outgoing, "tile", split_axis=0, concat_axis=2, tiled=True)
    row_tiles = received.shape[0]
    grouped = received.reshape(row_tiles, freq_dev, tile_rows, per_tile, 2, rank_max, sources)
    return jnp.sum(grouped.astype(jnp.float32), axis=3).astype(jnp.bfloat16)


def split_tiles_body(traces, right_basis, left_basis, tile_ranks):
    freq_count = lax.axis_size("freq")
    tile_count = lax.axis_size("tile")
    time_rows, grid_rows, sources = traces.shape
    freq_dev = right_basis.shape[0]
    total_time = time_rows * freq_count
    tile_rows = tile_ranks.shape[1]
    rank_max = right_basis.shape[2] // (2 * tile_rows)
    tile_points = grid_rows * tile_count // tile_rows
    freq_ids = 1 + jnp.arange(freq_count * freq_dev, dtype=jnp.int32)
    time_ids = lax.axis_index("freq") * time_rows + jnp.arange(time_rows, dtype=jnp.int32)
    twiddle = twiddles(freq_ids, time_ids, total_time)
    spectra = lax.psum_scatter(
        jnp.einsum("fpt,tns->fpns", twiddle, traces, preferred_element_type=jnp.float32).astype(
            jnp.bfloat16
        ),
        "freq",
        scatter_dimension=0,
        tiled=True,
    )
    piece_rows = min(tile_points, grid_rows)
    pieces_dev = grid_rows // piece_rows
    per_tile = max(tile_points // grid_rows, 1)
    spectra_pieces = spectra.reshape(freq_dev, 2, pieces_dev, piece_rows, sources)
    right_pieces = right_basis.reshape(freq_dev, pieces_dev, piece_rows, 2 * tile_rows * rank_max)
    products = jnp.einsum(
        "fqnc,fpqns->cfqps", right_pieces, spectra_pieces, preferred_element_type=jnp.float32
    )
    products = products.reshape(2, tile_rows, rank_max, freq_dev, pieces_dev, 2, sources)
    real_part = products[0, :, :, :, :, 0] - products[1, :, :, :, :, 1]
    imag_part = products[0, :, :, :, :, 1] + products[1, :, :, :, :, 0]
    stacked = jnp.transpose(jnp.stack([real_part, imag_part], 0), (1, 3, 4, 0, 2, 5))
    column_ids = (
        lax.axis_index("tile") * pieces_dev + jnp.arange(pieces_dev, dtype=jnp.int32)
    ) // per_tile
    onehot = (column_ids[:, None] == jnp.arange(tile_rows, dtype=jnp.int32)[None, :]).astype(
        jnp.int32
    )
    chosen = jnp.sum(tile_ranks[:, :, None, :] * onehot[None, None], axis=-1)
    keep_rows = jnp.arange(rank_max, dtype=jnp.int32)[None, None, None, :] < chosen[..., None]
    keep_rows = jnp.transpose(keep_rows, (1, 0, 2, 3))[:, :, :, None, :, None]
    rank_rows = jnp.where(keep_rows, stacked, jnp.float32(0.0)).astype(jnp.bfloat16)
    coupled = send_pieces(rank_rows, tile_count, tile_rows, per_tile)
    row_tiles = coupled.shape[0]
    rows_tile = grid_rows // row_tiles
    real_coupled = coupled[:, :, :, 0]
    imag_coupled = coupled[:, :, :, 1]
    upper_half = jnp.stack([real_coupled, imag_coupled], -2)
    lower_half = jnp.stack([-imag_coupled, real_coupled], -2)
    operand = jnp.stack([upper_half, lower_half], 2)
    left_tiles = left_basis.reshape(freq_dev, row_tiles, rows_tile, 2, tile_rows, rank_max)
    field_out = jnp.einsum(
        "frtajk,rfajkys->fyrts", left_tiles, operand, preferred_element_type=jnp.float32
    )
    return field_out.reshape(freq_dev, 2, grid_rows, sources).astype(jnp.bfloat16)


def pack_kernel(dims, off_ref, rank_ref, place_ref, right_ref, spec_ref, out_ref, own_ref, buf):
    peers, per_dev, rank, sources, cap, full = dims
    freq, col = pl.program_id(0), pl.program_id(1)
    half = peers * per_dev * rank
    real, imag = spec_ref[0, 0], spec_ref[0, 1]
    upper = jnp.concatenate([real, imag], axis=1)
    lower = jnp.concatenate([-imag, real], axis=1)
    rows = lax.broadcasted_iota(jnp.int32, (rank, 2 * sources), 0)
    contract = (((0,), (0,)), ((), ()))
    width = per_dev * rank
    for peer in range(peers):
        real_cols = right_ref[0, :, peer * width : (peer + 1) * width]
        imag_cols = right_ref[0, :, half + peer * width : half + (peer + 1) * width]
        total = lax.dot_general(real_cols, upper, contract, preferred_element_type=jnp.float32)
        total += lax.dot_general(imag_cols, lower, contract, preferred_element_type=jnp.float32)
        for row in range(per_dev):
            index = ((freq * per_dev + col) * peers + peer) * per_dev + row
            kept = jnp.where(rows < rank_ref[index], total[row * rank : (row + 1) * rank], 0.0)
            buf[0, peer, pl.ds(off_ref[index], rank), :] = kept[:, :sources]
            buf[1, peer, pl.ds(off_ref[index], rank), :] = kept[:, sources:]

    @pl.when((freq == pl.num_programs(0) - 1) & (col == pl.num_programs(1) - 1))
    def _():
        @pl.loop(0, peers)
        def _(peer):
            for part in range(2):
                lanes = slice(part * sources, (part + 1) * sources)
                out_ref[peer, :, lanes] = buf[part, peer, :cap, :].astype(out_ref.dtype)

        for part in range(2):
            lanes = slice(part * sources, (part + 1) * sources)
            own_ref[:, lanes] = buf[part, place_ref[0], :full, :].astype(own_ref.dtype)


def unpack_kernel(dims, off_ref, rank_ref, place_ref, recv_ref, own_ref, left_ref, out_ref, buf, operand):
    peers, per_dev, rank, sources, cap, full = dims
    freq, row = pl.program_id(0), pl.program_id(1)
    half = peers * per_dev * rank

    @pl.when((freq == 0) & (row == 0))
    def _():
        @pl.loop(0, peers)
        def _(peer):
            for part in range(2):
                lanes = slice(part * sources, (part + 1) * sources)
                buf[part, peer, :cap, :] = recv_ref[peer, :, lanes].astype(jnp.float32)

        for part in range(2):
            lanes = slice(part * sources, (part + 1) * sources)
            buf[part, place_ref[0], :full, :] = own_ref[:, lanes].astype(jnp.float32)

    rows = lax.broadcasted_iota(jnp.int32, (rank, sources), 0)

    @pl.loop(0, peers, unroll=2)
    def _(peer):
        for each in range(per_dev):
            col = peer * per_dev + each
            index = (freq * per_dev + row) * (peers * per_dev) + col
            window = pl.ds(off_ref[index], rank)
            keep = rows < rank_ref[index]
            real = jnp.where(keep, buf[0, peer, window, :], 0.0)
            imag = jnp.where(keep, buf[1, peer, window, :], 0.0)
            upper = pl.ds(pl.multiple_of(col * rank, rank), rank)
            lower = pl.ds(pl.multiple_of(half + col * rank, rank), rank)
            operand[upper, :sources] = real.astype(operand.dtype)
            operand[upper, sources:] = imag.astype(operand.dtype)
            operand[lower, :sources] = (-imag).astype(operand.dtype)
            operand[lower, sources:] = real.astype(operand.dtype)

    field = jnp.dot(left_ref[0], operand[...], preferred_element_type=jnp.float32)
    out_ref[0, 0] = field[:, :sources].astype(out_ref.dtype)
    out_ref[0, 1] = field[:, sources:].astype(out_ref.dtype)


def pack(dims, count, offsets, ranks, place, right_basis, spectra):
    peers, per_dev, rank, sources, cap, full = dims
    points = right_basis.shape[1] // per_dev
    width = right_basis.shape[2]
    return pl.pallas_call(
        functools.partial(pack_kernel, dims),
        out_shape=(
            jax.ShapeDtypeStruct((peers, cap, 2 * sources), jnp.bfloat16),
            jax.ShapeDtypeStruct((full, 2 * sources), jnp.bfloat16),
        ),
        grid_spec=pltpu.PrefetchScalarGridSpec(
            num_scalar_prefetch=3,
            grid=(count, per_dev),
            in_specs=[
                pl.BlockSpec((1, points, width), lambda f, j, o, r, place: (f + place[1], j, 0)),
                pl.BlockSpec((1, 2, points, sources), lambda f, j, *_: (f, 0, j, 0)),
            ],
            out_specs=[
                pl.BlockSpec((peers, cap, 2 * sources), lambda f, j, *_: (0, 0, 0)),
                pl.BlockSpec((full, 2 * sources), lambda f, j, *_: (0, 0)),
            ],
            scratch_shapes=[pltpu.VMEM((2, peers, full + rank, sources), jnp.float32)],
        ),
        compiler_params=pltpu.CompilerParams(vmem_limit_bytes=62 << 20),
        cost_estimate=pl.CostEstimate(
            flops=4 * count * per_dev * points * width * sources,
            bytes_accessed=2 * count * per_dev * points * width + 4 * peers * cap * sources,
            transcendentals=0,
        ),
        name="pack_rows",
    )(offsets, ranks, place, right_basis, spectra)


def unpack(dims, count, offsets, ranks, place, received, own, left_basis):
    peers, per_dev, rank, sources, cap, full = dims
    grid_rows, width = left_basis.shape[1:]
    points = grid_rows // per_dev
    return pl.pallas_call(
        functools.partial(unpack_kernel, dims),
        out_shape=jax.ShapeDtypeStruct((count, 2, grid_rows, sources), jnp.bfloat16),
        grid_spec=pltpu.PrefetchScalarGridSpec(
            num_scalar_prefetch=3,
            grid=(count, per_dev),
            in_specs=[
                pl.BlockSpec((peers, cap, 2 * sources), lambda f, i, *_: (0, 0, 0)),
                pl.BlockSpec((full, 2 * sources), lambda f, i, *_: (0, 0)),
                pl.BlockSpec((1, points, width), lambda f, i, o, r, place: (f + place[1], i, 0)),
            ],
            out_specs=pl.BlockSpec((1, 2, points, sources), lambda f, i, *_: (f, 0, i, 0)),
            scratch_shapes=[
                pltpu.VMEM((2, peers, full + rank, sources), jnp.float32),
                pltpu.VMEM((width, 2 * sources), jnp.bfloat16),
            ],
        ),
        compiler_params=pltpu.CompilerParams(vmem_limit_bytes=62 << 20),
        cost_estimate=pl.CostEstimate(
            flops=4 * count * grid_rows * width * sources,
            bytes_accessed=2 * count * grid_rows * width + 4 * peers * cap * sources,
            transcendentals=0,
        ),
        name="apply_left",
    )(offsets, ranks, place, received, own, left_basis)


def tile_order(ranks, peers, per_dev):
    count = ranks.shape[0]
    split = ranks.reshape(count, peers, per_dev, peers, per_dev)
    return jnp.transpose(split, (3, 1, 0, 4, 2)).reshape(peers, peers, count * per_dev * per_dev)


def partial_spectra(first, count, freq_dev, traces):
    freq_count = lax.axis_size("freq")
    time_rows = traces.shape[0]
    time_ids = lax.axis_index("freq") * time_rows + jnp.arange(time_rows, dtype=jnp.int32)
    freq_ids = (
        1
        + jnp.arange(freq_count, dtype=jnp.int32)[:, None] * freq_dev
        + (first + jnp.arange(count, dtype=jnp.int32))[None, :]
    ).reshape(freq_count * count)
    return jnp.einsum(
        "fpt,tns->fpns",
        twiddles(freq_ids, time_ids, time_rows * freq_count),
        traces,
        preferred_element_type=jnp.float32,
    ).astype(jnp.bfloat16)


def scatter_spectra(partial_sums):
    return lax.psum_scatter(partial_sums, "freq", scatter_dimension=0, tiled=True)


def tables(first, count, packed, tile_ranks, peers, per_dev, rank):
    ranks = lax.dynamic_slice_in_dim(tile_ranks, first, count, axis=0)
    ranks = tile_order(ranks, peers, per_dev)
    if packed:
        offsets = jnp.cumsum(ranks, axis=2) - ranks
    else:
        offsets = jnp.broadcast_to(jnp.arange(ranks.shape[2], dtype=jnp.int32) * rank, ranks.shape)
    me = lax.axis_index("tile").astype(jnp.int32)

    def outgoing(table):
        mine = lax.dynamic_index_in_dim(table, me, 0, keepdims=False)
        mine = mine.reshape(peers, count, per_dev, per_dev)
        return jnp.transpose(mine, (1, 2, 0, 3)).reshape(-1)

    def incoming(table):
        mine = lax.dynamic_index_in_dim(table, me, 1, keepdims=False)
        mine = mine.reshape(peers, count, per_dev, per_dev)
        return jnp.transpose(mine, (1, 3, 0, 2)).reshape(-1)

    place = jnp.stack([me, jnp.asarray(first, jnp.int32)])
    sending = (outgoing(offsets), outgoing(ranks), place)
    receiving = (incoming(offsets), incoming(ranks), place)
    return sending, receiving


def exchange(sent):
    return lax.all_to_all(sent, "tile", split_axis=0, concat_axis=0, tiled=True)


def body(traces, right_basis, left_basis, tile_ranks):
    peers = lax.axis_size("tile")
    tile_rows = tile_ranks.shape[1]
    if tile_rows % peers != 0:
        return split_tiles_body(traces, right_basis, left_basis, tile_ranks)
    freq_dev = right_basis.shape[0]
    sources = traces.shape[2]
    per_dev = tile_rows // peers
    rank = right_basis.shape[2] // (2 * tile_rows)
    tiles = per_dev * per_dev

    def capacity(count):
        lowest = max(rank // 8, 1)
        mean = (lowest + rank) / 2
        spread = math.sqrt(((rank - lowest + 1) ** 2 - 1) / 12)
        rows = mean * count * tiles + 4.1 * spread * math.sqrt(count * tiles)
        return min(-(-int(rows) // 16) * 16, count * tiles * rank)

    counts = [1] + [2] * ((freq_dev - 2) // 2) + [1] * (1 + freq_dev % 2)
    if freq_dev < 2:
        counts = [1] * freq_dev
    starts = [sum(counts[:n]) for n in range(len(counts))]
    chunks = list(zip(starts, counts))

    elsewhere = ~jnp.eye(peers, dtype=bool)
    over = jnp.int32(0)
    for first, count in chunks:
        totals = jnp.sum(tile_order(tile_ranks[first : first + count], peers, per_dev), axis=2)
        over = over | jnp.any((totals > capacity(count)) & elsewhere).astype(jnp.int32)
    over = lax.pmax(over, "freq")

    spectra = scatter_spectra(partial_spectra(*chunks[0], freq_dev, traces))
    where = tables(*chunks[0], True, tile_ranks, peers, per_dev, rank)[0]
    following = None
    if len(chunks) > 1:
        following = partial_spectra(*chunks[1], freq_dev, traces)
        spectra, following, where = lax.optimization_barrier((spectra, following, where))

    def fast(spectra, following, where, traces, right_basis, left_basis, tile_ranks):
        fields = []
        own, received, last = None, None, None

        def apply_last(last, received):
            dims, count, receiving, own = last
            return unpack(dims, count, *receiving, received, own, left_basis)

        for n, (first, count) in enumerate(chunks):
            dims = (peers, per_dev, rank, sources, capacity(count), count * tiles * rank)
            sending, receiving = tables(first, count, True, tile_ranks, peers, per_dev, rank)
            if n == 0:
                sending = where
            else:
                sending, _ = lax.optimization_barrier((sending, own))
            upcoming = None
            if n + 1 < len(chunks):
                upcoming = scatter_spectra(following)
            sent, own = pack(dims, count, *sending, right_basis, spectra)
            if n > 0:
                sent, received = lax.optimization_barrier((sent, received))
                fields.append(apply_last(last, received))
            received = exchange(sent)
            if n + 2 < len(chunks):
                following = partial_spectra(*chunks[n + 2], freq_dev, traces)
                upcoming, following = lax.optimization_barrier((upcoming, following))
            spectra = upcoming
            last = (dims, count, receiving, own)
        fields.append(apply_last(last, received))
        return jnp.concatenate(fields, axis=0)

    def complete(spectra, following, where, traces, right_basis, left_basis, tile_ranks):
        full = tiles * rank
        dims = (peers, per_dev, rank, sources, full, full)

        def one(carry, first):
            sending, receiving = tables(first, 1, False, tile_ranks, peers, per_dev, rank)
            spectra = scatter_spectra(partial_spectra(first, 1, freq_dev, traces))
            sent, own = pack(dims, 1, *sending, right_basis, spectra)
            field = unpack(dims, 1, *receiving, exchange(sent), own, left_basis)
            return carry, field[0]

        return lax.scan(one, 0, jnp.arange(freq_dev, dtype=jnp.int32))[1]

    return lax.cond(
        over == 0, fast, complete, spectra, following, where, traces, right_basis, left_basis, tile_ranks
    )


def solution(mesh):
    return jax.shard_map(
        body,
        mesh=mesh,
        in_specs=(
            P("freq", "tile", None),
            P("freq", "tile", None),
            P("freq", "tile", None),
            P("freq", None, None),
        ),
        out_specs=P("freq", None, "tile", None),
        check_vma=False,
    )
```
